32 devices in a mesh: tok: 4 (over y, x), hid: 8 (over z, core).
Axes of the slice: x: 2, y: 2, z: 4, core: 2. Of those that a mesh axis runs over, the one named last changes fastest.
Arguments:
- activations: bfloat16 [4096, 4096], P('tok', 'hid'), may hold values from -6 to 6
- gate_weight: bfloat16 [4096, 14336], P(None, 'hid'), may hold values from -0.09375 to 0.09375
- up_weight: bfloat16 [4096, 14336], P(None, 'hid'), may hold values from -0.09375 to 0.09375
- row_signs: int32 [4096], P('tok'), may hold values from 0 to 1
- row_scales: float32 [4096], P('tok'), may hold values from 0.25 to 4
- kept_rows: int32 [256], P('tok'), may hold values from 0 to 1023, as said below
Outputs:
- gram_matrix: float32 [256, 256], P('tok')
The draws below stay inside these ranges and needn't reach their ends.
Inputs may be any that keep to these rules, and one draw needn't show every extreme that they name: `kept_rows`: within each aligned block of 64 entries the values are distinct.
All inputs are finite; a program needn't handle non-finite values.
Results may differ from the reference program's by a relative error of at most 0.0014.
Values may be sent and summed in bfloat16 or wider, within the bound.
No kernel may reach another device: no remote copies, remote signals or barrier semaphores. Data moves between devices by JAX's collectives and lax.ppermute only.
A program may use at most 128 MiB of HBM per device.

```python
import math
import jax
import jax.numpy as jnp
from jax import lax

D = 4096
FF = 14336
TOK_DEV = 1024
KEPT = 64
TOKENS = 4096
KEPT_TOTAL = 256


def draw_kept_rows(key, part):
    shard_keys = jax.random.split(key, KEPT_TOTAL // KEPT)
    chosen = jax.vmap(lambda single: jax.random.permutation(single, TOK_DEV)[:KEPT])(shard_keys)
    return chosen.reshape(KEPT_TOTAL).astype(jnp.int32)


def touch_ends(result, rng, least, high):
    dims = result.shape
    spot = [jax.random.randint(jax.random.fold_in(rng, axis), (), 0, dims[axis]) for axis in range(len(dims))]
    result = result.at[tuple(spot)].set(least)
    longest = dims.index(max(dims))
    spot[longest] = (spot[longest] + 1) % dims[longest]
    return result.at[tuple(spot)].set(high)


def level_of(key, extent, pieces, low, top_value):
    def one(axis_at, shards_of):
        draws = jax.random.uniform(jax.random.fold_in(jax.random.fold_in(key, 6), axis_at), (shards_of,), jnp.float32, low / len(pieces), top_value / len(pieces))
        return jnp.repeat(jnp.exp(draws), extent[axis_at] // shards_of).reshape((-1,) + (1,) * (len(extent) - axis_at - 1))

    loudness = one(*pieces[0])
    for cut in pieces[1:]:
        loudness = loudness * one(*cut)
    return loudness


def bell_draw(own_key, shape, deviation, most, shards=(), held_as=jnp.bfloat16):
    entries = jax.random.normal(own_key, shape, jnp.float32) * deviation
    if len(shards) > 0:
        entries = level_of(own_key, shape, shards, -0.22, 0.18) * entries
    return jnp.clip(entries, min=-most, max=most).astype(held_as)


def setup_inputs(seed: int = 0) -> dict:
    key_list = jax.random.split(jax.random.key(seed), 7)
    activations = bell_draw(key_list[0], (TOKENS, D), 1.0, 6.0, ((0, 4), (1, 8)))
    gate_weight = bell_draw(key_list[1], (D, FF), D ** -0.5, 0.09375, ((1, 8),))
    up_weight = bell_draw(key_list[2], (D, FF), D ** -0.5, 0.09375, ((1, 8),))
    row_signs = touch_ends(jax.random.randint(key_list[3], (TOKENS,), 0, 2), jax.random.fold_in(key_list[3], 1), 0, 1).astype(jnp.int32)
    row_scales = jnp.clip(jnp.exp(math.log(4.0) - 2.7725887 * jax.random.uniform(key_list[4], (TOKENS,), jnp.float32) ** level_of(key_list[4], (TOKENS,), ((0, 4),), -0.2, 0.2)), 0.25, 4.0)
    kept_rows = draw_kept_rows(jax.random.fold_in(key_list[6], 71), 0)
    return dict(activations=activations, gate_weight=gate_weight, up_weight=up_weight, row_signs=row_signs, row_scales=row_scales, kept_rows=kept_rows)


def bit_parity(values):
    parity = jnp.zeros_like(values)
    for shift_count in range(16):
        parity = parity ^ ((values >> shift_count) & 1)
    return parity


def hadamard_signs(first_rows, columns):
    parity = bit_parity(first_rows[:, None] & columns[None, :])
    return 1 - 2 * parity


def reference(activations, gate_weight, up_weight, row_signs, row_scales, kept_rows):
    gate_proj = jnp.dot(activations, gate_weight, preferred_element_type=jnp.float32)
    up_proj = jnp.dot(activations, up_weight, preferred_element_type=jnp.float32)
    row_factor = (2 * row_signs - 1).astype(jnp.float32) * row_scales
    signed_hidden = (row_factor[:, None] * jax.nn.silu(gate_proj) * up_proj).astype(jnp.bfloat16)
    shard_count = KEPT_TOTAL // KEPT
    blocks = signed_hidden.astype(jnp.float32).reshape(shard_count, TOK_DEV, FF)
    inner_table = hadamard_signs(jnp.arange(TOK_DEV, dtype=jnp.int32), jnp.arange(TOK_DEV, dtype=jnp.int32)).astype(jnp.float32)
    outer_table = hadamard_signs(jnp.arange(shard_count, dtype=jnp.int32), jnp.arange(shard_count, dtype=jnp.int32)).astype(jnp.float32)
    local_rows = jnp.einsum('kl,jlf->jkf', inner_table, blocks, precision=lax.Precision.HIGHEST)
    transformed = jnp.einsum('ij,jkf->ikf', outer_table, local_rows, precision=lax.Precision.HIGHEST)
    transformed = transformed.reshape(TOKENS, FF) * (float(TOKENS) ** -0.5)
    picked = (jnp.arange(KEPT_TOTAL, dtype=jnp.int32) // KEPT) * TOK_DEV + kept_rows.astype(jnp.int32)
    sketch = transformed[picked].astype(jnp.bfloat16)
    gram_matrix = jnp.dot(sketch, sketch.T, preferred_element_type=jnp.float32) * (float(FF) ** -0.5)
    return gram_matrix
```

```python
import functools

import jax
import jax.numpy as jnp
from jax import lax
from jax.experimental import pallas as pl
from jax.experimental.pallas import tpu as pltpu
from jax.sharding import PartitionSpec as P

F32, BF16 = jnp.float32, jnp.bfloat16
VMEM = pl.BlockSpec(memory_space=pltpu.VMEM)
SMEM = pl.BlockSpec(memory_space=pltpu.SMEM)
HBM = pl.BlockSpec(memory_space=pltpu.HBM)


def parity_signs(rows, columns):
    bits = rows[:, None] & columns[None, :]
    for shift in (16, 8, 4, 2, 1):
        bits = bits ^ (bits >> shift)
    return 1 - 2 * (bits & 1)


def column_tile(columns):
    for tile in (896, 512, 256, 128):
        if columns % tile == 0:
            return tile
    return columns


def weight_copies(index, gate, up, buffer, sem, depth, tile, step, slot):
    columns = pl.ds(pl.multiple_of(step * tile, tile), tile)
    return [
        pltpu.make_async_copy(
            weight.at[pl.ds(pl.multiple_of(index[half] * depth, depth), depth), columns],
            buffer.at[slot, which, pl.ds(half * depth, depth)],
            sem.at[slot, which, half],
        )
        for which, weight in enumerate((gate, up))
        for half in range(2)
    ]


def over_tiles(index, gate, up, buffer, sem, depth, tile, count, work):
    args = (index, gate, up, buffer, sem, depth, tile)
    for copy in weight_copies(*args, 0, 0):
        copy.start()

    def step(tile_index, carry):
        slot = lax.rem(tile_index, 2)

        @pl.when(tile_index + 1 < count)
        def _():
            for copy in weight_copies(*args, tile_index + 1, 1 - slot):
                copy.start()

        for copy in weight_copies(*args, tile_index, slot):
            copy.wait()
        work(slot, pl.ds(pl.multiple_of(tile_index * tile, tile), tile))
        return carry

    lax.fori_loop(0, count, step, 0)


def product(near, far, buffer, slot, which, depth):
    return jnp.dot(
        near[...], buffer[slot, which, :depth], preferred_element_type=F32
    ) + jnp.dot(far[...], buffer[slot, which, depth:], preferred_element_type=F32)


def first_kernel(tile, index, near, far, gate, up, total, buffer, sem):
    depth = near.shape[1]

    def work(slot, columns):
        for which in range(2):
            total[which, :, columns] = product(near, far, buffer, slot, which, depth)

    over_tiles(index, gate, up, buffer, sem, depth, tile, total.shape[2] // tile, work)


def more_kernel(tile, index, near, far, before, gate, up, total, buffer, sem):
    depth = near.shape[1]

    def work(slot, columns):
        for which in range(2):
            total[which, :, columns] = before[which, :, columns] + product(
                near, far, buffer, slot, which, depth
            )

    over_tiles(index, gate, up, buffer, sem, depth, tile, total.shape[2] // tile, work)


def accumulate(index, near, far, gate, up, before=None):
    rows, depth = near.shape
    columns = gate.shape[1]
    tile = column_tile(columns)
    kernel = first_kernel if before is None else more_kernel
    held = [] if before is None else [before]
    return pl.pallas_call(
        functools.partial(kernel, tile),
        out_shape=jax.ShapeDtypeStruct((2, rows, columns), F32),
        in_specs=[SMEM, VMEM, VMEM] + [VMEM] * len(held) + [HBM, HBM],
        out_specs=VMEM,
        scratch_shapes=[
            pltpu.VMEM((2, 2, 2 * depth, tile), BF16),
            pltpu.SemaphoreType.DMA((2, 2, 2)),
        ],
        input_output_aliases={3: 0} if held else {},
        compiler_params=pltpu.CompilerParams(vmem_limit_bytes=24 << 20),
        cost_estimate=pl.CostEstimate(
            flops=8 * rows * depth * columns, bytes_accessed=8 * depth * columns, transcendentals=0
        ),
    )(index, near, far, *held, gate, up)


def finish_kernel(tile, offset, held, index, near, far, before, factor, signs, *refs):
    depth = near.shape[1]
    rows = near.shape[0]
    if held:
        part_in, gate, up, part, buffer, sem = refs
    else:
        gate, up, part, buffer, sem = refs

    def work(slot, columns):
        span = pl.ds(offset, rows)
        gate_proj = before[0, span, columns] + product(near, far, buffer, slot, 0, depth)
        up_proj = before[1, span, columns] + product(near, far, buffer, slot, 1, depth)
        hidden = factor[...] * (gate_proj / (1 + jnp.exp(-gate_proj))) * up_proj
        rows_part = jnp.dot(signs[...], hidden.astype(BF16), preferred_element_type=F32)
        part[:, columns] = rows_part + part_in[:, columns] if held else rows_part

    over_tiles(index, gate, up, buffer, sem, depth, tile, before.shape[2] // tile, work)


def finish(index, near, far, before, offset, factor, signs, gate, up, part=None):
    rows, depth = near.shape
    columns = gate.shape[1]
    kept = signs.shape[0]
    tile = 256 if columns % 256 == 0 else columns
    held = [] if part is None else [part]
    return pl.pallas_call(
        functools.partial(finish_kernel, tile, offset, bool(held)),
        out_shape=jax.ShapeDtypeStruct((kept, columns), F32),
        in_specs=[SMEM] + [VMEM] * (5 + len(held)) + [HBM, HBM],
        out_specs=VMEM,
        scratch_shapes=[
            pltpu.VMEM((2, 2, 2 * depth, tile), BF16),
            pltpu.SemaphoreType.DMA((2, 2, 2)),
        ],
        input_output_aliases={6: 0} if held else {},
        compiler_params=pltpu.CompilerParams(vmem_limit_bytes=24 << 20),
        cost_estimate=pl.CostEstimate(
            flops=8 * rows * depth * columns + 2 * kept * rows * columns,
            bytes_accessed=8 * depth * columns,
            transcendentals=rows * columns,
        ),
    )(index, near, far, before, factor, signs, *held, gate, up)


def swap_pairs(count, mask):
    return [(place, place ^ mask) for place in range(count)]


def line_pairs(pairs, parity, step):
    moves = []
    for place in range(pairs):
        upward = place % 2 == parity
        other = place + 1 if upward else place - 1
        block = place + step if upward else place - step
        if 0 <= other < pairs and 0 <= block < pairs:
            moves += [(2 * other + core, 2 * place + core) for core in range(2)]
    return moves


def tokens_exchanged(values, shards, position):
    rows = values.shape[0] // shards

    def block(mask):
        return lax.dynamic_slice_in_dim(values, (position ^ mask) * rows, rows, 0)

    moved = [
        lax.ppermute(block(mask), "tok", swap_pairs(shards, mask)) for mask in range(1, shards)
    ]
    total = block(0).astype(F32)
    for piece in moved:
        total = total + piece.astype(F32)
    return total


def line_device(activations, gate_weight, up_weight, row_signs, row_scales, kept_rows):
    tok_rows, depth = activations.shape
    shards = lax.axis_size("tok")
    hid = lax.axis_size("hid")
    pairs = hid // 2
    position = lax.axis_index("tok")
    place = lax.axis_index("hid")
    line, core = place // 2, place % 2
    even = line % 2 == 0
    half = tok_rows // 2

    def over_hid(values, moves):
        return lax.ppermute(values, "hid", moves)

    def twin(values):
        return over_hid(values, swap_pairs(hid, 1))

    every = [kept_rows] + [
        lax.ppermute(kept_rows, "tok", swap_pairs(shards, mask)) for mask in range(1, shards)
    ]
    every = jnp.stack(every)[jnp.arange(shards) ^ position]
    kept = kept_rows.shape[0] * shards
    every = (every + tok_rows * jnp.arange(shards, dtype=jnp.int32)[:, None]).reshape(kept)
    local = position * tok_rows + jnp.arange(tok_rows, dtype=jnp.int32)
    signs = parity_signs(every, local).astype(BF16)
    factor = ((2 * row_signs - 1).astype(F32) * row_scales)[:, None]

    halves = [activations[:half], activations[half:]]
    even_got = {1: [over_hid(part, line_pairs(pairs, 0, 1)) for part in halves]}
    odd_got = {1: [over_hid(part, line_pairs(pairs, 1, 1)) for part in halves]}
    blocks = [line]
    arrived = [even_got[1]]
    toward = jnp.where(even, 1, -1)
    blocks.append(line + toward)
    for step in range(2, pairs):
        even_got[step] = [over_hid(part, line_pairs(pairs, 0, step)) for part in odd_got[step - 1]]
        if step < pairs - 1:
            odd_got[step] = [
                over_hid(part, line_pairs(pairs, 1, step)) for part in even_got[step - 1]
            ]
        ahead = line + toward * step
        valid = (ahead >= 0) & (ahead < pairs)
        arrived.append(
            [jnp.where(valid, e, o) for e, o in zip(even_got[step], odd_got[step - 1])]
        )
        blocks.append(jnp.where(valid, ahead, line - toward * (step - 1)))

    def index_of(block):
        return jnp.stack([2 * block + core, 2 * block + 1 - core]).astype(jnp.int32)

    weights = (gate_weight, up_weight)
    own_twin = twin(activations)
    totals = [
        accumulate(index_of(line), halves[s], own_twin[s * half : (s + 1) * half], *weights)
        for s in range(2)
    ]
    for step in range(pairs - 2):
        for s in range(2):
            near = arrived[step][s]
            totals[s] = accumulate(
                index_of(blocks[step + 1]), near, twin(near), *weights, totals[s]
            )
    part = None
    for s in range(2):
        near = arrived[-1][s]
        rows = slice(s * half, (s + 1) * half)
        part = finish(
            index_of(blocks[-1]), near, twin(near), totals[s], 0,
            factor[rows], signs[:, rows], *weights, part,
        )

    turned = part.T.astype(BF16)
    columns = gate_weight.shape[1]
    scale = float(tok_rows * shards) ** -0.5
    sketch = (tokens_exchanged(turned, shards, position) * scale).astype(BF16)
    gram = lax.dot_general(
        sketch, sketch, (((0,), (0,)), ((), ())), preferred_element_type=F32
    ) * (float(columns * hid) ** -0.5)
    total = tokens_exchanged(gram, shards, position)
    moved = [over_hid(total, swap_pairs(hid, 2 * mask)) for mask in range(1, pairs)]
    for piece in moved:
        total = total + piece
    return total + twin(total)


def gather_device(activations, gate_weight, up_weight, row_signs, row_scales, kept_rows):
    tok_rows = activations.shape[0]
    shards = lax.axis_size("tok")
    position = lax.axis_index("tok")
    columns = gate_weight.shape[1] * lax.axis_size("hid")
    whole = lax.all_gather(activations, "hid", axis=1, tiled=True)
    gate_proj = jnp.dot(whole, gate_weight, preferred_element_type=F32)
    up_proj = jnp.dot(whole, up_weight, preferred_element_type=F32)
    factor = (2 * row_signs - 1).astype(F32) * row_scales
    hidden = (factor[:, None] * jax.nn.silu(gate_proj) * up_proj).astype(BF16)
    every = lax.all_gather(kept_rows, "tok", axis=0, tiled=True)
    owner = jnp.arange(every.shape[0], dtype=jnp.int32) // kept_rows.shape[0]
    local = position * tok_rows + jnp.arange(tok_rows, dtype=jnp.int32)
    signs = parity_signs(owner * tok_rows + every, local).astype(BF16)
    part = jnp.dot(signs, hidden, preferred_element_type=F32)
    mine = lax.psum_scatter(part, "tok", scatter_dimension=0, tiled=True)
    sketch = (mine * float(tok_rows * shards) ** -0.5).astype(BF16)
    gram = lax.dot_general(
        sketch,
        lax.all_gather(sketch, "tok", axis=0, tiled=True),
        (((1,), (1,)), ((), ())),
        preferred_element_type=F32,
    )
    return lax.psum(gram * float(columns) ** -0.5, "hid")


def solution(mesh):
    short = mesh.shape["hid"] % 2 == 0 and 2 < mesh.shape["hid"] // 2 <= 4
    placed = (P("tok", "hid"), P(None, "hid"), P(None, "hid"), P("tok"), P("tok"), P("tok"))
    return jax.shard_map(
        line_device if short else gather_device,
        mesh=mesh,
        in_specs=placed,
        out_specs=P("tok", None),
        check_vma=False,
    )
```
